256 devices in a mesh: seq: 32 (over y_lo, z, core), head: 8 (over x, y_hi).
Axes of the slice: x: 4, y: 4 (y_hi: 2, y_lo: 2; y = y_hi * 2 + y_lo), z: 8, core: 2. Of those that a mesh axis runs over, the one named last changes fastest.
Arguments:
- queries: bfloat16 [12288, 3072], P('seq', 'head'), may hold values from -56 to 56, as said below
- keys: bfloat16 [12288, 3072], P('seq', 'head'), may hold values from -4 to 4, as said below
- values: bfloat16 [12288, 3072], P('seq', 'head'), may hold values from -6 to 6
- out_weight: bfloat16 [3072, 3072], P('head'), may hold values from -0.109375 to 0.109375
- residual: bfloat16 [12288, 3072], P(('seq', 'head')), may hold values from -6 to 6
- gate: float32 [3072], replicated, may hold values from 0.5 to 2
Outputs:
- mixed: bfloat16 [12288, 3072], P(('seq', 'head'))
The draws below stay inside these ranges and needn't reach their ends.
Inputs may be any that keep to these rules, and one draw needn't show every extreme that they name: `queries`: query entries of the attention. `keys`: key entries of the attention.
All inputs are finite; a program needn't handle non-finite values.
Results may differ from the reference program's by a relative error of at most 0.0075.
Values may be sent and summed in bfloat16 or wider, within the bound.
No kernel may reach another device: no remote copies, remote signals or barrier semaphores. Data moves between devices by JAX's collectives and lax.ppermute only.
A program may use at most 192 MiB of HBM per device.

```python
import math
import jax
import jax.numpy as jnp
from jax import lax

D = 3072
HEADS = 24
HD = 128
TOK_DEV = 384
TOKENS = 12288
N_SEQ = 32


def key_table(key):
    table = jnp.clip(jax.random.normal(jax.random.fold_in(key, 7), (TOKENS, HEADS * HD), jnp.float32), -4.0, 4.0)
    return table


def draw_keys(key, part):
    return key_table(key).astype(jnp.bfloat16)


def draw_queries(key, part):
    base = jnp.clip(3.5 * jax.random.normal(jax.random.fold_in(key, 11), (TOKENS, HEADS * HD), jnp.float32), -14.0, 14.0)
    return base.astype(jnp.bfloat16)


def levels(rng, shape, split, least, top_value):
    level, own = 1.0, jax.random.fold_in(rng, 6)
    for axis_at, shards_of in split:
        draws = jnp.exp(jax.random.uniform(jax.random.fold_in(own, axis_at), (shards_of,), jnp.float32, least / len(split), top_value / len(split)))
        level = level * jnp.repeat(draws, shape[axis_at] // shards_of).reshape([-1 if axis == axis_at else 1 for axis in range(len(shape))])
    return level


def scatter_about(rng, dims, width, most, pieces=(), kind=jnp.bfloat16):
    factor_of = levels(rng, dims, pieces, -0.22, 0.18) if pieces else 1.0
    values = jax.random.normal(rng, dims, jnp.float32) * width * factor_of
    return jnp.minimum(jnp.maximum(values, -most), most).astype(kind)


def setup_inputs(seed: int = 0) -> dict:
    key_list = jax.random.split(jax.random.key(seed), 7)
    queries = draw_queries(jax.random.fold_in(key_list[6], 71), 0)
    keys = draw_keys(jax.random.fold_in(key_list[6], 71), 0)
    values = scatter_about(key_list[2], (TOKENS, HEADS * HD), 1.0, 6.0, ((0, 32), (1, 8)))
    out_weight = scatter_about(key_list[3], (HEADS * HD, D), (HEADS * HD) ** -0.5, 0.109375, ((0, 8),))
    residual = scatter_about(key_list[4], (TOKENS, D), 1.0, 6.0, ((0, 256),))
    gate = jnp.clip(jnp.exp(jax.random.uniform(key_list[5], (D,), jnp.float32, math.log(0.5), math.log(2.0))), 0.5, 2.0)
    return {"queries": queries, "keys": keys, "values": values, "out_weight": out_weight, "residual": residual, "gate": gate}


def reference(queries, keys, values, out_weight, residual, gate):
    scale = 1.0 / (HD ** 0.5)
    key_all = keys.reshape(TOKENS, HEADS, HD).astype(jnp.float32)
    value_all = values.reshape(TOKENS, HEADS, HD).astype(jnp.float32)
    query_blocks = queries.reshape(N_SEQ, TOK_DEV, HEADS, HD)

    def attend(query_block):
        scores = jnp.einsum("qhd,khd->hqk", query_block.astype(jnp.float32), key_all) * scale
        highest = jnp.max(scores, axis=-1, keepdims=True)
        expd = jnp.exp(scores - highest)
        totals = jnp.sum(expd, axis=-1)
        probs = lax.optimization_barrier(expd.astype(jnp.bfloat16)).astype(jnp.float32)
        summed = jnp.einsum("hqk,khd->qhd", probs, value_all)
        return (summed / jnp.transpose(totals)[:, :, None]).astype(jnp.bfloat16)

    attention = lax.map(attend, query_blocks).reshape(TOKENS, HEADS * HD)
    projected = jnp.dot(attention, out_weight, preferred_element_type=jnp.float32)
    return (residual.astype(jnp.float32) + gate * projected).astype(jnp.bfloat16)
```

```python
import functools

import jax
import jax.numpy as jnp
from jax import lax
from jax.experimental import pallas as pl
from jax.experimental.pallas import tpu as pltpu
from jax.sharding import PartitionSpec as P

HD = 128
TOK = 384
LANES = 3 * HD
QT = 256
PACK = LANES + 16
SCALE = float(HD**-0.5 * 1.4426950408889634)
NT = (((1,), (1,)), ((), ()))
F32, BF16 = jnp.float32, jnp.bfloat16


def seq_of(y, z, c):
    return (y * 8 + z) * 2 + c


ALL = [(y, z, c) for y in range(2) for z in range(8) for c in range(2)]


def along_z(d):
    return [(seq_of(y, z, c), seq_of(y, (z + d) % 8, c)) for y, z, c in ALL]


def to_partner(dy, dc):
    return [(seq_of(y, z, c), seq_of(y ^ dy, z, c ^ dc)) for y, z, c in ALL]


def along_x(d):
    pairs = []
    for y, z, c in ALL:
        for x in range(4):
            for h in range(2):
                to = (x + (d if c == 0 else -d)) % 4
                pairs.append((seq_of(y, z, c) * 8 + x * 2 + h, seq_of(y, z, c) * 8 + to * 2 + h))
    return pairs


HALF_SWAP = [(x * 2 + h, x * 2 + 1 - h) for x in range(4) for h in range(2)]
VMEM = pl.BlockSpec(memory_space=pltpu.VMEM)


def call(kernel, outs, args, scratch=(), aliases=None, flops=0, exps=0, name=None, limit=24 << 20):
    moved = sum(a.size * a.dtype.itemsize for a in args)
    return pl.pallas_call(
        kernel,
        out_shape=outs,
        in_specs=[VMEM] * len(args),
        out_specs=jax.tree.map(lambda _: VMEM, outs),
        scratch_shapes=list(scratch),
        input_output_aliases=aliases or {},
        cost_estimate=pl.CostEstimate(flops=flops, bytes_accessed=moved, transcendentals=exps),
        compiler_params=pltpu.CompilerParams(vmem_limit_bytes=limit),
        name=name,
    )(*args)


def split3(v):
    hi = v.astype(BF16)
    rest = v - hi.astype(F32)
    mid = rest.astype(BF16)
    return hi, mid, (rest - mid.astype(F32)).astype(BF16)


def attend_kernel(kind, first, last, tile0, tiles, unroll, *refs):
    n_kv = 1 if kind == "one" else 2
    q_ref, kvs, refs = refs[0], refs[1 : 1 + n_kv], refs[1 + n_kv :]
    if not first:
        st_in, acc_in, refs = refs[0], refs[1], refs[2:]
    if last:
        out, s_scr, p_scr = refs
    else:
        st, acc, s_scr, p_scr = refs
    n_keys = s_scr.shape[1]
    ones = jnp.ones((16, n_keys), BF16)

    def cols(i):
        return pl.ds(i * QT, QT) if isinstance(i, int) else pl.ds(pl.multiple_of(i * QT, QT), QT)

    def scores(i, h, slot):
        q = q_ref[cols(i), h * HD : (h + 1) * HD]
        at = 0
        for kv in kvs:
            n = kv.shape[0]
            s_scr[slot, at : at + n, :] = lax.dot_general(
                kv[:, h * HD : (h + 1) * HD], q, NT, preferred_element_type=F32
            )
            at += n

    def values_t(h):
        lo, hi = h * HD, (h + 1) * HD
        if kind == "halves":
            half = TOK // 2
            parts = []
            if lo < half:
                parts.append(kvs[0][lo : min(hi, half), LANES:])
            if hi > half:
                parts.append(kvs[1][max(lo - half, 0) : hi - half, LANES:])
            return parts
        return [jnp.concatenate([kv[lo:hi, LANES:] for kv in kvs], 1)]

    def soften(i, h, slot):
        m1 = jnp.max(s_scr[slot], axis=0, keepdims=True)
        alpha = None
        if not first:
            m0 = st_in[h : h + 1, cols(i)]
            m1 = jnp.maximum(m0, m1)
            alpha = jnp.exp2(m0 * SCALE - m1 * SCALE)
        mc = m1 * SCALE
        p_scr[slot] = jnp.exp2(s_scr[slot] * SCALE - mc).astype(BF16)
        if not last:
            st[h : h + 1, cols(i)] = m1
        return alpha, mc

    def gather(i, h, slot, alpha, mc):
        o = jnp.dot(jnp.concatenate(values_t(h) + [ones], 0), p_scr[slot], preferred_element_type=F32)
        total, o = o[HD : HD + 1], o[:HD]
        rows = slice(h * HD, (h + 1) * HD)
        if not first:
            total = st_in[3 + h : 4 + h, cols(i)] * alpha + total
            o = acc_in[rows, cols(i)] * alpha + o
        if last:
            c = slice((i - tile0) * QT, (i - tile0 + 1) * QT)
            out[rows, c] = (o / total).astype(BF16)
            return mc + jnp.log2(total)
        acc[rows, cols(i)] = o
        st[3 + h : 4 + h, cols(i)] = total

    def finish(i, logs):
        c = slice((i - tile0) * QT, (i - tile0 + 1) * QT)
        parts = [split3(v) for v in logs]
        rows = [p[j] for j in range(3) for p in parts]
        rows.append(jnp.zeros((7, QT), BF16))
        out[LANES:, c] = jnp.concatenate(rows, 0)

    if last:
        todo = [(i, h) for i in range(tile0, tile0 + tiles) for h in range(3)]
        scores(*todo[0], 0)
        before, logs = None, []
        for t, (i, h) in enumerate(todo + [(None, None)]):
            if t + 1 < len(todo):
                scores(*todo[t + 1], (t + 1) % 2)
            now = None
            if i is not None:
                now = (i, h, t % 2, *soften(i, h, t % 2))
            if before is not None:
                logs.append(gather(*before))
                if len(logs) == 3:
                    finish(before[0], logs)
                    logs = []
            before = now
        return
    n = 3 * unroll
    scores(tile0, 0, 0)

    def body(g, carry):
        before = None
        for t in range(n):
            i, h = tile0 + g * unroll + t // 3, t % 3
            i2, h2 = tile0 + g * unroll + (t + 1) // 3, (t + 1) % 3
            if t + 1 == n:
                i2 = jnp.minimum(i2, tile0 + tiles - 1)
            scores(i2, h2, (t + 1) % 2)
            now = (i, h, t % 2, *soften(i, h, t % 2))
            if before is not None:
                gather(*before)
            before = now
        gather(*before)
        return carry

    lax.fori_loop(0, tiles // unroll, body, 0)


def attend(kind, q, kvs, state=None, part=None):
    first, last = state is None, part is not None
    n_keys = 768 if kind == "two" else 384
    rows = q.shape[0]
    tile0, tiles = (part * 3, 3) if last else (0, rows // QT)
    args = [q, *kvs] + ([] if first else list(state))
    aliases = None
    if last:
        outs = jax.ShapeDtypeStruct((PACK, tiles * QT), BF16)
    else:
        outs = (jax.ShapeDtypeStruct((8, rows), F32), jax.ShapeDtypeStruct((LANES, rows), F32))
        if not first:
            aliases = {len(args) - 2: 0, len(args) - 1: 1}
    kernel = functools.partial(attend_kernel, kind, first, last, tile0, tiles, 2)
    return call(
        kernel,
        outs,
        args,
        [pltpu.VMEM((2, n_keys, QT), F32), pltpu.VMEM((2, n_keys, QT), BF16)],
        aliases,
        4 * tiles * QT * n_keys * LANES,
        3 * tiles * QT * n_keys,
        "attend",
    )


def logs_of(block, h):
    r = [block[LANES + 3 * j + h : LANES + 3 * j + h + 1].astype(F32) for j in range(3)]
    return r[0] + r[1] + r[2]


def joined(a, b, tail):
    outs, logs = [], []
    ta, tb = a[LANES:], b[LANES:]
    for h in range(3):
        la = ta[h : h + 1].astype(F32) + ta[3 + h : 4 + h].astype(F32) + ta[6 + h : 7 + h].astype(F32)
        lb = tb[h : h + 1].astype(F32) + tb[3 + h : 4 + h].astype(F32) + tb[6 + h : 7 + h].astype(F32)
        top = jnp.maximum(la, lb)
        wa, wb = jnp.exp2(la - top), jnp.exp2(lb - top)
        total = wa + wb
        rows = slice(h * HD, (h + 1) * HD)
        outs.append(a[rows].astype(F32) * (wa / total) + b[rows].astype(F32) * (wb / total))
        if tail:
            logs.append(top + jnp.log2(total))
    return outs, logs


def join_kernel(at, a_ref, b_ref, out):
    c = slice(at, at + TOK)
    outs, logs = joined(a_ref[:, c], b_ref[:, c], True)
    for h in range(3):
        out[h * HD : (h + 1) * HD, :] = outs[h].astype(BF16)
    parts = [split3(v) for v in logs]
    rows = [p[j] for j in range(3) for p in parts] + [jnp.zeros((7, TOK), BF16)]
    out[LANES:, :] = jnp.concatenate(rows, 0)


def spread_kernel(a_ref, b_ref, own, near, far, across, scr):
    outs, _ = joined(a_ref[...], b_ref[...], False)
    for h in range(3):
        scr[:, h * HD : (h + 1) * HD] = outs[h].T.astype(BF16)
    x = lax.axis_index("head") // 2
    core = lax.axis_index("seq") % 2
    step = 1 - 2 * core
    n = TOK // 4
    for ref, d in ((own, 0), (near, step), (far, 4 - step), (across, 2)):
        to = lax.rem(x + d + 4, 4)
        ref[...] = scr[pl.ds(pl.multiple_of(to * n, n), n), :]


def project_kernel(a0, a1, a2, a3, w0, w1, w2, w3m, w3t, keep, send, scr):
    half = lax.axis_index("head") % 2
    core = lax.axis_index("seq") % 2
    n = keep.shape[0]

    def turned(ref):
        return jnp.concatenate(
            [ref[pl.ds(pl.multiple_of((1 - half) * n, n), n), :], ref[pl.ds(pl.multiple_of(half * n, n), n), :]], 0
        )

    rows = [turned(a) for a in (a0, a1, a2, a3)]
    width = w3m.shape[1]

    def piece(j, w3):
        c = slice(j * width, (j + 1) * width)
        total = jnp.dot(rows[3], w3[...], preferred_element_type=F32)
        for a, w in zip(rows, (w0, w1, w2)):
            total += jnp.dot(a, w[:, c], preferred_element_type=F32)
        send[:, c] = total[:n].astype(BF16)
        keep[:, c] = total[n:]

    for c in range(2):

        @pl.when(core == c)
        def _():
            piece(0, w3m if c == 0 else w3t)
            piece(1, w3t if c == 0 else w3m)


def local(queries, keys, values, out_weight, residual, gate):
    core = lax.axis_index("seq") % 2
    width = out_weight.shape[1]
    block = jnp.concatenate([keys, values.T], axis=1)
    up, down = block, block
    ups, downs = [], []
    for _ in range(3):
        up = lax.ppermute(up, "seq", along_z(1))
        down = lax.ppermute(down, "seq", along_z(-1))
        ups.append(up)
        downs.append(down)
    opposite = (
        lax.ppermute(up[: TOK // 2], "seq", along_z(1)),
        lax.ppermute(down[TOK // 2 :], "seq", along_z(-1)),
    )
    q_y = lax.ppermute(queries, "seq", to_partner(1, 0))
    q_c = lax.ppermute(queries, "seq", to_partner(0, 1))
    q_yc = lax.ppermute(q_y, "seq", to_partner(0, 1))
    q = jnp.concatenate([queries, q_y, q_c, q_yc], axis=0)

    both = ("seq", "head")
    w_near = lax.ppermute(out_weight, both, along_x(1))
    w_half = lax.dynamic_slice_in_dim(w_near, core * (width // 2), width // 2, axis=1)
    w_across = lax.ppermute(w_half, both, along_x(1))
    w_far = lax.ppermute(w_near, "seq", to_partner(0, 1))
    w_across2 = lax.ppermute(w_across, "seq", to_partner(0, 1))

    state = attend("one", q, [block])
    for s in range(3):
        state = attend("two", q, [ups[s], downs[s]], state)
    given = attend("halves", q, opposite, state, part=1)
    got = lax.ppermute(given, "seq", to_partner(0, 1))
    kept = attend("halves", q, opposite, state, part=0)

    packed = jax.ShapeDtypeStruct((PACK, TOK), BF16)
    for_y = call(functools.partial(join_kernel, TOK), packed, [kept, got], name="join")
    from_y = lax.ppermute(for_y, "seq", to_partner(1, 0))
    mine = call(functools.partial(join_kernel, 0), packed, [kept, got], name="join")
    quarter = jax.ShapeDtypeStruct((TOK // 4, LANES), BF16)
    a0, a1, a2, a3 = call(
        spread_kernel, (quarter,) * 4, [mine, from_y], [pltpu.VMEM((TOK, LANES), BF16)], name="spread"
    )
    a1 = lax.ppermute(a1, both, along_x(1))
    a2 = lax.ppermute(a2, both, along_x(-1))
    a3 = lax.ppermute(a3, both, along_x(2))
    n = TOK // 8
    keep, send = call(
        project_kernel,
        (jax.ShapeDtypeStruct((n, width), F32), jax.ShapeDtypeStruct((n, width), BF16)),
        [a0, a1, a2, a3, out_weight, w_near, w_far, w_across, w_across2],
        [pltpu.VMEM((8, 128), F32)],
        flops=2 * 2 * n * 4 * LANES * width,
        name="project",
    )
    other = lax.ppermute(send, "head", HALF_SWAP)
    projected = keep + other.astype(F32)
    return (residual.astype(F32) + gate * projected).astype(BF16)


def solution(mesh):
    placed = (
        P("seq", "head"),
        P("seq", "head"),
        P("seq", "head"),
        P("head", None),
        P(("seq", "head"), None),
        P(),
    )
    return jax.shard_map(
        local, mesh=mesh, in_specs=placed, out_specs=P(("seq", "head"), None), check_vma=False
    )
```

```python
import functools

import jax
import jax.numpy as jnp
from jax import lax
from jax.experimental import pallas as pl
from jax.experimental.pallas import tpu as pltpu
from jax.sharding import PartitionSpec as P

HD = 128
TOK = 384
LANES = 3 * HD
QT = 256
PACK = LANES + 16
SCALE = float(HD**-0.5 * 1.4426950408889634)
NT = (((1,), (1,)), ((), ()))
F32, BF16 = jnp.float32, jnp.bfloat16


def seq_of(y, z, c):
    return (y * 8 + z) * 2 + c


ALL = [(y, z, c) for y in range(2) for z in range(8) for c in range(2)]


def along_z():
    return [(seq_of(y, z, c), seq_of(y, (z + 1 - 2 * c) % 8, c)) for y, z, c in ALL]


def to_partner(dy, dc):
    return [(seq_of(y, z, c), seq_of(y ^ dy, z, c ^ dc)) for y, z, c in ALL]


def along_x(d):
    pairs = []
    for y, z, c in ALL:
        for x in range(4):
            for h in range(2):
                to = (x + (d if c == 0 else -d)) % 4
                pairs.append((seq_of(y, z, c) * 8 + x * 2 + h, seq_of(y, z, c) * 8 + to * 2 + h))
    return pairs


HALF_SWAP = [(x * 2 + h, x * 2 + 1 - h) for x in range(4) for h in range(2)]
VMEM = pl.BlockSpec(memory_space=pltpu.VMEM)


def call(kernel, outs, args, scratch=(), aliases=None, flops=0, exps=0, limit=12 << 20):
    moved = sum(a.size * a.dtype.itemsize for a in args)
    return pl.pallas_call(
        kernel,
        out_shape=outs,
        in_specs=[VMEM] * len(args),
        out_specs=jax.tree.map(lambda _: VMEM, outs),
        scratch_shapes=list(scratch),
        input_output_aliases=aliases or {},
        cost_estimate=pl.CostEstimate(flops=flops, bytes_accessed=moved, transcendentals=exps),
        compiler_params=pltpu.CompilerParams(vmem_limit_bytes=limit),
    )(*args)


def split3(v):
    hi = v.astype(BF16)
    rest = v - hi.astype(F32)
    mid = rest.astype(BF16)
    return hi, mid, (rest - mid.astype(F32)).astype(BF16)


def side_kernel(k_ref, v_ref, out, sems):
    copies = [
        pltpu.make_async_copy(ref, out.at[:, j * LANES : (j + 1) * LANES], sems.at[j])
        for j, ref in enumerate((k_ref, v_ref))
    ]
    for c in copies:
        c.start()
    for c in copies:
        c.wait()


def side_by_side(keys, values):
    return pl.pallas_call(
        side_kernel,
        out_shape=jax.ShapeDtypeStruct((TOK, 2 * LANES), BF16),
        in_specs=[pl.BlockSpec(memory_space=pltpu.HBM)] * 2,
        out_specs=VMEM,
        scratch_shapes=[pltpu.SemaphoreType.DMA((2,))],
        compiler_params=pltpu.CompilerParams(vmem_limit_bytes=4 << 20),
        name="side",
    )(keys, values)


def attend_kernel(n_q, n_kv, first, last, qt, part, *refs):
    qs, kvs, refs = refs[:n_q], refs[n_q : n_q + n_kv], refs[n_q + n_kv :]
    if not first:
        st_in, acc_in, refs = refs[0], refs[1], refs[2:]
    if last:
        out, s_scr, p_scr, v_scr = refs
    elif n_q > 1:
        q_ref, st, acc, s_scr, p_scr, v_scr = refs
        for j, q in enumerate(qs):
            q_ref[j * TOK : (j + 1) * TOK, :] = q[...]
    else:
        st, acc, s_scr, p_scr, v_scr = refs
    if n_q == 1:
        q_ref = qs[0]
    tiles = 4 * TOK // qt
    n_keys = s_scr.shape[1]
    ones = jnp.ones((16, n_keys), BF16)
    at = 0
    for kv in kvs:
        v_scr[:, at : at + kv.shape[0]] = kv[:, LANES:].T
        at += kv.shape[0]

    def cols(i):
        return pl.ds(i * qt, qt) if isinstance(i, int) else pl.ds(pl.multiple_of(i * qt, qt), qt)

    def scores(i, h, slot):
        q = q_ref[cols(i), h * HD : (h + 1) * HD]
        at = 0
        for kv in kvs:
            n = kv.shape[0]
            s_scr[slot, at : at + n, :] = lax.dot_general(
                kv[:, h * HD : (h + 1) * HD], q, NT, preferred_element_type=F32
            )
            at += n

    def soften(i, h, slot):
        m1 = jnp.max(s_scr[slot], axis=0, keepdims=True)
        alpha = None
        if not first:
            m0 = st_in[h : h + 1, cols(i)]
            m1 = jnp.maximum(m0, m1)
            alpha = jnp.exp2(m0 * SCALE - m1 * SCALE)
        mc = m1 * SCALE
        p_scr[slot] = jnp.exp2(s_scr[slot] * SCALE - mc).astype(BF16)
        if not last:
            st[h : h + 1, cols(i)] = m1
        return alpha, mc

    def gather(i, h, slot, alpha, mc):
        o = jnp.dot(
            jnp.concatenate([v_scr[h * HD : (h + 1) * HD], ones], 0), p_scr[slot], preferred_element_type=F32
        )
        total, o = o[HD : HD + 1], o[:HD]
        rows = slice(h * HD, (h + 1) * HD)
        if not first:
            total = st_in[3 + h : 4 + h, cols(i)] * alpha + total
            o = acc_in[rows, cols(i)] * alpha + o
        if last:
            out[rows, :] = (o / total).astype(BF16)
            return mc + jnp.log2(total)
        acc[rows, cols(i)] = o
        st[3 + h : 4 + h, cols(i)] = total

    if last:
        scores(part, 0, 0)
        before, logs = None, []
        for h in range(4):
            if h < 2:
                scores(part, h + 1, (h + 1) % 2)
            now = (part, h, h % 2, *soften(part, h, h % 2)) if h < 3 else None
            if before is not None:
                logs.append(gather(*before))
            before = now
        out[LANES:, :] = packed_logs(logs)
        return
    n = 6
    scores(0, 0, 0)

    def body(g, carry):
        before = None
        for t in range(n):
            i, h = g * 2 + t // 3, t % 3
            i2, h2 = g * 2 + (t + 1) // 3, (t + 1) % 3
            if t + 1 == n:
                i2 = jnp.minimum(i2, tiles - 1)
            scores(i2, h2, (t + 1) % 2)
            now = (i, h, t % 2, *soften(i, h, t % 2))
            if before is not None:
                gather(*before)
            before = now
        gather(*before)
        return carry

    lax.fori_loop(0, tiles // 2, body, 0)


def attend(qs, kvs, state=None, part=None):
    first, last = state is None, part is not None
    n_keys = sum(kv.shape[0] for kv in kvs)
    rows = 4 * TOK
    qt = TOK if last else QT
    args = [*qs, *kvs] + ([] if first else list(state))
    aliases = None
    if last:
        outs = jax.ShapeDtypeStruct((PACK, TOK), BF16)
    else:
        outs = (jax.ShapeDtypeStruct((8, rows), F32), jax.ShapeDtypeStruct((LANES, rows), F32))
        if len(qs) > 1:
            outs = (jax.ShapeDtypeStruct((rows, LANES), BF16), *outs)
        if not first:
            aliases = {len(args) - 2: 0, len(args) - 1: 1}
    kernel = functools.partial(attend_kernel, len(qs), len(kvs), first, last, qt, part)
    work = n_keys * LANES * (TOK if last else rows)
    return call(
        kernel,
        outs,
        args,
        [
            pltpu.VMEM((2, n_keys, qt), F32),
            pltpu.VMEM((2, n_keys, qt), BF16),
            pltpu.VMEM((LANES, n_keys), BF16),
        ],
        aliases,
        4 * work,
        work // HD,
    )


def packed_logs(logs):
    parts = [split3(v) for v in logs]
    rows = [p[j] for j in range(3) for p in parts]
    return jnp.concatenate(rows + [jnp.zeros((7, rows[0].shape[1]), BF16)], 0)


def logs_of(tail, h):
    return sum(tail[3 * j + h : 3 * j + h + 1].astype(F32) for j in range(3))


def weights(tail_a, tail_b, h):
    la, lb = logs_of(tail_a, h), logs_of(tail_b, h)
    top = jnp.maximum(la, lb)
    wa, wb = jnp.exp2(la - top), jnp.exp2(lb - top)
    total = wa + wb
    return wa / total, wb / total, top + jnp.log2(total)


def joined(a, b, h):
    rows = slice(h * HD, (h + 1) * HD)
    wa, wb, log = weights(a[LANES:, :], b[LANES:, :], h)
    return a[rows, :].astype(F32) * wa + b[rows, :].astype(F32) * wb, log


def join_kernel(a_ref, b_ref, out):
    logs = []
    for h in range(3):
        total, log = joined(a_ref, b_ref, h)
        out[h * HD : (h + 1) * HD, :] = total.astype(BF16)
        logs.append(log)
    out[LANES:, :] = packed_logs(logs)


def spread_kernel(a_ref, b_ref, *refs):
    outs, scr = refs[:4], refs[4]
    for h in range(3):
        scr[:, h * HD : (h + 1) * HD] = joined(a_ref, b_ref, h)[0].T.astype(BF16)
    x = lax.axis_index("head") // 2
    step = 1 - 2 * (lax.axis_index("seq") % 2)
    n = TOK // 4
    for ref, d in zip(outs, (0, step, 4 - step, 2)):
        to = lax.rem(x + d + 4, 4)
        ref[...] = scr[pl.ds(pl.multiple_of(to * n, n), n), :]


def project_kernel(*refs):
    pieces, (w0, w1, w2, w3m, w3t, keep, send) = refs[:4], refs[4:]
    half = lax.axis_index("head") % 2
    core = lax.axis_index("seq") % 2
    n = keep.shape[0]

    def halves(i):
        return jnp.concatenate(
            [pieces[i][pl.ds(pl.multiple_of(h * n, n), n), :] for h in (1 - half, half)], 0
        )

    att = [halves(i) for i in range(4)]
    width = w3m.shape[1]

    def piece(j, w3):
        c = slice(j * width, (j + 1) * width)
        total = jnp.dot(att[3], w3[...], preferred_element_type=F32)
        for a, w in zip(att, (w0, w1, w2)):
            total += jnp.dot(a, w[:, c], preferred_element_type=F32)
        send[:, c] = total[:n].astype(BF16)
        keep[:, c] = total[n:]

    for c in range(2):

        @pl.when(core == c)
        def _():
            piece(0, w3m if c == 0 else w3t)
            piece(1, w3t if c == 0 else w3m)


def body(queries, keys, values, out_weight, residual, gate):
    core = lax.axis_index("seq") % 2
    width = out_weight.shape[1]
    both = ("seq", "head")
    swap, cross = to_partner(0, 1), to_partner(1, 0)
    barrier = lax.optimization_barrier
    block = side_by_side(keys, values)

    def hop(x):
        return lax.ppermute(x, "seq", along_z())

    a1 = hop(block)
    partner = lax.ppermute(block, "seq", swap)
    b1 = hop(partner)
    q_y = lax.ppermute(queries, "seq", cross)
    q_c = lax.ppermute(queries, "seq", swap)
    q_yc = lax.ppermute(q_y, "seq", swap)
    w_near = lax.ppermute(out_weight, both, along_x(1))
    a2 = hop(a1)
    q, *state = attend([queries, q_y, q_c, q_yc], [block, a1])
    b2 = hop(b1)
    a2, *state = barrier((a2, *state))
    a3 = hop(a2)
    state = attend([q], [b1, a2], state)
    b2, w_near, *state = barrier((b2, w_near, *state))
    b3 = hop(b2)
    w_half = lax.dynamic_slice_in_dim(w_near, core * (width // 2), width // 2, axis=1)
    w_across = lax.ppermute(w_half, both, along_x(1))
    w_far = lax.ppermute(w_near, "seq", swap)
    a4 = hop(a3)
    state = attend([q], [b2, a3], state)
    b3, *state = barrier((b3, *state))
    state = attend([q], [b3], state)
    a4, w_across, *state = barrier((a4, w_across, *state))
    w_across2 = lax.ppermute(w_across, "seq", swap)
    last = [a4]

    give_y = attend([q], last, state, part=3)
    got_y = lax.ppermute(give_y, "seq", swap)
    keep_y = attend([q], last, state, part=1)
    give_own = attend([q], last, state, part=2)
    got_own = lax.ppermute(give_own, "seq", swap)
    packed = jax.ShapeDtypeStruct((PACK, TOK), BF16)
    from_y = lax.ppermute(call(join_kernel, packed, [keep_y, got_y]), "seq", cross)
    keep_own = attend([q], last, state, part=0)
    mine = call(join_kernel, packed, [keep_own, got_own])
    quarter = jax.ShapeDtypeStruct((TOK // 4, LANES), BF16)
    a0, a1, a2, a3 = call(
        spread_kernel, (quarter,) * 4, [mine, from_y], [pltpu.VMEM((TOK, LANES), BF16)]
    )
    a1 = lax.ppermute(a1, both, along_x(1))
    a2 = lax.ppermute(a2, both, along_x(-1))
    a3 = lax.ppermute(a3, both, along_x(2))
    n = TOK // 8
    keep, send = call(
        project_kernel,
        (jax.ShapeDtypeStruct((n, width), F32), jax.ShapeDtypeStruct((n, width), BF16)),
        [a0, a1, a2, a3, out_weight, w_near, w_far, w_across, w_across2],
        flops=2 * 2 * n * 4 * LANES * width,
        limit=18 << 20,
    )
    other = lax.ppermute(send, "head", HALF_SWAP)
    projected = keep + other.astype(F32)
    return (residual.astype(F32) + gate * projected).astype(BF16)


def solution(mesh):
    placed = (
        P("seq", "head"),
        P("seq", "head"),
        P("seq", "head"),
        P("head", None),
        P(("seq", "head"), None),
        P(),
    )
    return jax.shard_map(
        body, mesh=mesh, in_specs=placed, out_specs=P(("seq", "head"), None), check_vma=False
    )
```
